32 devices in a mesh: dp: 16 (over z, x, core), seq: 2 (over y).
Axes of the slice: x: 2, y: 2, z: 4, core: 2. Of those that a mesh axis runs over, the one named last changes fastest.
Arguments:
- inputs: bfloat16 [2, 16, 256, 768], P(None, 'dp', 'seq'), may hold values from -6 to 6
- cotangent: bfloat16 [2, 16, 256, 768], P(None, 'dp', 'seq'), may hold values from -6 to 6
- w_qkv: float32 [1769472], P(('dp', 'seq')), may hold values from -0.21875 to 0.21875
- w_out: float32 [589824], P(('dp', 'seq')), may hold values from -0.21875 to 0.21875
- w_fc1: float32 [2359296], P(('dp', 'seq')), may hold values from -0.21875 to 0.21875
- w_fc2: float32 [2359296], P(('dp', 'seq')), may hold values from -0.109375 to 0.109375
- vectors: float32 [11520], P(('dp', 'seq')), may hold values from -0.9 to 1.5, as said below
- offsets: int32 [3, 12], replicated, may hold values from 0 to 3, as said below
Outputs:
- layer_out: bfloat16 [2, 16, 256, 768], P(None, 'dp', 'seq')
- input_grad: float32 [2, 16, 256, 768], P(None, 'dp', 'seq')
- grad_qkv: float32 [1769472], P(('dp', 'seq'))
- grad_out: float32 [589824], P(('dp', 'seq'))
- grad_fc1: float32 [2359296], P(('dp', 'seq'))
- grad_fc2: float32 [2359296], P(('dp', 'seq'))
- grad_vectors: float32 [11520], P(('dp', 'seq'))
The draws below stay inside these ranges and needn't reach their ends.
Inputs may be any that keep to these rules, and one draw needn't show every extreme that they name: `offsets`: row b (b = 0, 1, 2) holds every head's offset below the dilation 1, 2, 4 of branch b; each value below a branch's dilation is held by 12 divided by that dilation heads. `vectors`: the four gains lie in 0.5 to 1.5; the biases lie in -0.9 to 0.9.
All inputs are finite; a program needn't handle non-finite values.
Results may differ from the reference program's by a relative error of at most 0.012.
The reference program's roundings to bfloat16 on the way count: a program that leaves them out, or rounds other values in their place, can miss the bound.
Values may be sent and summed in bfloat16 or wider, within the bound.
A program may use at most 192 MiB of HBM per device.

```python
import jax
import jax.numpy as jnp
from jax import lax

D = 768
HEADS = 12
FF = 3072
HEAD_DIM = 64
MB = 2
SEQS = 16
SEQ_LEN = 256


def draw_vectors(key, part):
    piece_sizes = (D, D, D, D, D, D, FF, FF, D)
    gain_pieces = (0, 3, 5, 7)
    pieces = []
    for piece_index in range(9):
        piece_key = jax.random.fold_in(key, 11 + piece_index)
        piece_len = piece_sizes[piece_index]
        if piece_index in gain_pieces:
            pieces.append(jax.random.uniform(piece_key, (piece_len,), jnp.float32, 0.5, 1.5))
        else:
            normal_vals = jax.random.normal(piece_key, (piece_len,), jnp.float32)
            pieces.append(0.3 * jnp.clip(normal_vals, -3.0, 3.0))
    return jnp.concatenate(pieces)


def draw_offsets(key, part):
    offset_rows = []
    for branch in range(3):
        dilate = (1, 2, 4)[branch]
        shuffled = jax.random.permutation(jax.random.fold_in(key, 101 + branch), HEADS)
        offset_rows.append((shuffled % dilate).astype(jnp.int32))
    return jnp.stack(offset_rows)


def block_scale(key, extent, cuts, smallest, high):
    gain = 1.0
    for axis_at, shards_of in cuts:
        steps = jax.random.uniform(jax.random.fold_in(jax.random.fold_in(key, 6), axis_at), (shards_of,), jnp.float32, smallest / len(cuts), high / len(cuts))
        gain = gain * jnp.repeat(jnp.exp(steps), extent[axis_at] // shards_of).reshape((-1,) + (1,) * (len(extent) - 1 - axis_at))
    return gain


def gaussian(own_key, extent, width, limit, shards=(), held_as=jnp.bfloat16):
    values = jax.random.normal(own_key, extent, jnp.float32) * width
    if len(shards) > 0:
        values = block_scale(own_key, extent, shards, -0.22, 0.18) * values
    return jnp.clip(values, min=-limit, max=limit).astype(held_as)


def setup_inputs(seed: int = 0) -> dict:
    arg_keys = jax.random.split(jax.random.key(seed), 9)
    return {
        "inputs": gaussian(arg_keys[0], (MB, SEQS, SEQ_LEN, D), 1.0, 6.0, ((1, 16), (2, 2))),
        "cotangent": gaussian(arg_keys[1], (MB, SEQS, SEQ_LEN, D), 1.0, 6.0, ((1, 16), (2, 2))),
        "w_qkv": gaussian(arg_keys[2], (3 * D * D,), D ** -0.5, 0.21875, ((0, 32),), jnp.float32),
        "w_out": gaussian(arg_keys[3], (D * D,), D ** -0.5, 0.21875, ((0, 32),), jnp.float32),
        "w_fc1": gaussian(arg_keys[4], (D * FF,), D ** -0.5, 0.21875, ((0, 32),), jnp.float32),
        "w_fc2": gaussian(arg_keys[5], (FF * D,), FF ** -0.5, 0.109375, ((0, 32),), jnp.float32),
        "vectors": draw_vectors(jax.random.fold_in(arg_keys[8], 71), 0),
        "offsets": draw_offsets(jax.random.fold_in(arg_keys[8], 71), 0),
    }


@jax.custom_vjp
def low(v):
    return lax.optimization_barrier(v.astype(jnp.bfloat16)).astype(jnp.float32)

@jax.custom_vjp
def low_back(v):
    return v

def low_keep(v):
    return (low(v), None)

def low_pass(kept, grad):
    return (grad,)

def back_keep(v):
    return (v, None)

def back_low(kept, grad):
    return (low(grad),)
low.defvjp(low_keep, low_pass)
low_back.defvjp(back_keep, back_low)
EPSILON = 1e-05
NEGATIVE = -1e+30
DILATIONS = (1, 2, 4)
SPANS = (4, 2, 1)

def matmul(left_op, right_op):
    return jnp.dot(left_op, right_op, precision=lax.Precision.HIGHEST, preferred_element_type=jnp.float32)

def layer_norm(features, gain_vec):
    row_mean = lax.optimization_barrier(jnp.mean(features, axis=-1, keepdims=True))
    centred = features - row_mean
    row_var = lax.optimization_barrier(jnp.mean(centred * centred, axis=-1, keepdims=True))
    return centred * lax.rsqrt(row_var + EPSILON) * gain_vec

def split_vectors(vectors):
    piece_sizes = (D, D, D, D, D, D, FF, FF, D)
    pieces = []
    position = 0
    for piece_len in piece_sizes:
        pieces.append(vectors[position:position + piece_len])
        position = position + piece_len
    return pieces

def head_mix(packed):
    head_query, head_keys, head_values, head_offsets = packed
    seq_rows = head_query.shape[0]
    score_scale = HEAD_DIM ** (-0.5)
    branch_outs = []
    branch_logs = []
    for branch in range(3):
        dilate = DILATIONS[branch]
        sparse_rows = seq_rows // dilate
        span_rows = seq_rows // SPANS[branch] // dilate
        chosen = (jnp.arange(dilate, dtype=jnp.int32) == head_offsets[branch]).astype(jnp.float32)

        def pick_rows(dense_rows):
            return lax.optimization_barrier(jnp.sum(dense_rows.reshape(sparse_rows, dilate, HEAD_DIM) * chosen[None, :, None], axis=1))
        scores = low_back(matmul(pick_rows(head_query), pick_rows(head_keys).T) * score_scale)
        row_ids = jnp.arange(sparse_rows, dtype=jnp.int32)[:, None]
        col_ids = jnp.arange(sparse_rows, dtype=jnp.int32)[None, :]
        allowed = (col_ids <= row_ids) & (col_ids // span_rows == row_ids // span_rows)
        scores = jnp.where(allowed, scores, NEGATIVE)
        log_sums = jax.nn.logsumexp(scores, axis=1)
        probability = jnp.exp(scores - log_sums[:, None])
        result = low_back(matmul(low(probability), pick_rows(head_values)))
        branch_outs.append((result[:, None, :] * chosen[None, :, None]).reshape(seq_rows, HEAD_DIM))
        branch_logs.append(jnp.where(chosen[None, :] > 0, log_sums[:, None], NEGATIVE).reshape(seq_rows))
    stacked = jnp.stack(branch_logs)
    total_log = jax.nn.logsumexp(stacked, axis=0)
    mixing = jnp.exp(stacked - total_log[None, :])
    return sum((mixing[branch][:, None] * branch_outs[branch] for branch in range(3)))

def forward(tokens, w_qkv, w_out, w_fc1, w_fc2, vectors, offsets):
    qkv_weight = low(w_qkv).reshape(D, 3 * D)
    out_weight = low(w_out).reshape(D, D)
    up_weight = low(w_fc1).reshape(D, FF)
    down_weight = low(w_fc2).reshape(FF, D)
    gain_in, bias_query, bias_value, gain_attn, bias_out, gain_mid, bias_up, gain_ffn, bias_down = split_vectors(low(vectors))
    seq_rows = tokens.shape[0]
    normed = low(layer_norm(tokens, gain_in))
    projected = matmul(normed, qkv_weight)
    queries = low(low_back(projected[:, :D] + bias_query))
    dense_keys = low(low_back(projected[:, D:2 * D]))
    dense_values = low(low_back(projected[:, 2 * D:] + bias_value))

    def by_heads(dense_rows):
        return dense_rows.reshape(seq_rows, HEADS, HEAD_DIM).transpose(1, 0, 2)
    mixed = lax.map(jax.checkpoint(head_mix), (by_heads(queries), by_heads(dense_keys), by_heads(dense_values), offsets.T))
    mixed = mixed.transpose(1, 0, 2).reshape(seq_rows, D)
    inner = low(layer_norm(mixed, gain_attn))
    middle = tokens + low_back(matmul(inner, out_weight) + bias_out)
    normed_mid = low(layer_norm(middle, gain_mid))
    hidden = low_back(matmul(normed_mid, up_weight) + bias_up)
    inner_ffn = low(layer_norm(jax.nn.gelu(hidden, approximate=False), gain_ffn))
    return middle + low_back(matmul(inner_ffn, down_weight) + bias_down)

def reference(inputs, cotangent, w_qkv, w_out, w_fc1, w_fc2, vectors, offsets):
    params = (w_qkv, w_out, w_fc1, w_fc2, vectors)
    seq_inputs = inputs.reshape(MB * SEQS, SEQ_LEN, D).astype(jnp.float32)
    seq_cotangent = cotangent.reshape(MB * SEQS, SEQ_LEN, D).astype(jnp.float32)

    def layer_apply(tokens_in, qkv_in, out_in, up_in, down_in, vector_in):
        return forward(tokens_in, qkv_in, out_in, up_in, down_in, vector_in, offsets)

    def one_sequence(totals, sequence):
        tokens, grad_seq = sequence
        result, pullback = jax.vjp(layer_apply, tokens, w_qkv, w_out, w_fc1, w_fc2, vectors)
        grad_list = pullback(grad_seq)
        summed = tuple((total_sum + grad_one for total_sum, grad_one in zip(totals, grad_list[1:])))
        return (summed, (result.astype(jnp.bfloat16), grad_list[0]))
    zeros = tuple((jnp.zeros_like(master) for master in params))
    totals, (layer_rows, grad_rows) = lax.scan(one_sequence, zeros, (seq_inputs, seq_cotangent))
    layer_out = layer_rows.reshape(MB, SEQS, SEQ_LEN, D)
    input_grad = grad_rows.reshape(MB, SEQS, SEQ_LEN, D)
    return (layer_out, input_grad, totals[0], totals[1], totals[2], totals[3], totals[4])
```

```python
from functools import partial

import jax
import jax.numpy as jnp
from jax import lax
from jax.experimental import pallas as pl
from jax.experimental.pallas import tpu as pltpu
from jax.sharding import PartitionSpec as P

D = 768
HEADS = 12
FF = 3072
HEAD_DIM = 64
TOK_BLK = 128
MB = 2

MESH = pl.DeviceIdType.MESH

def coords():
    dp = lax.axis_index("dp"); y = lax.axis_index("seq")
    return dp // 4, (dp // 2) % 2, dp % 2, y

def dev(z, x, c, y):
    return (z * 4 + x * 2 + c, y)

def slab(z, x, c, y):
    return z * 8 + x * 4 + c * 2 + y

def ag_body(nw, order, srcs, outs, send_sem, recv_sem, loc_sem):
    z, x, c, y = coords()
    barrier = pltpu.get_barrier_semaphore()
    def sig(d):
        pl.semaphore_signal(barrier, inc=1, device_id=d, device_id_type=MESH)
    sig(dev(z, 1 - x, c, y)); sig(dev(z, x, 1 - c, y)); sig(dev(z, x, c, 1 - y))
    @pl.when(z > 0)
    def _(): sig(dev(z - 1, x, c, y))
    @pl.when(z < 3)
    def _(): sig(dev(z + 1, x, c, y))
    pl.semaphore_wait(barrier, 3 + (z + 2) // 3 + (5 - z) // 3)

    me = slab(z, x, c, y)
    def cp(w, s, k, d):
        own = outs[w].at[s]
        return pltpu.make_async_remote_copy(src_ref=own, dst_ref=own,
            send_sem=send_sem.at[w, k], recv_sem=recv_sem.at[w, s], device_id=d, device_id_type=MESH)
    def waitr(w, s):
        own = outs[w].at[s]
        pltpu.make_async_remote_copy(src_ref=own, dst_ref=own,
            send_sem=send_sem.at[w, 0], recv_sem=recv_sem.at[w, s], device_id=dev(z, 1 - x, c, y), device_id_type=MESH).wait_recv()
    pend = []
    def go(w, s, k, d, cond=None):
        if cond is None:
            cp(w, s, k, d).start()
        else:
            @pl.when(cond)
            def _(): cp(w, s, k, d).start()
        pend.append((w, s, k, d, cond))
    xn, yn, cn = dev(z, 1 - x, c, y), dev(z, x, c, 1 - y), dev(z, x, 1 - c, y)
    zr, zl = dev(lax.min(z + 1, 3), x, c, y), dev(lax.max(z - 1, 0), x, c, y)
    def core(w, s, cond=None):
        go(w, s, 8 + (s // 4) * 2 + s % 2, cn, cond)
    def col(w, zz, right, left, cond=None):
        s = slab(zz, x, c, y)
        if right is not None: go(w, s, 24 + zz, zr, right)
        if left is not None: go(w, s, 28 + zz, zl, left)
        go(w, s, 0 + zz, xn, cond)
        go(w, s, 4 + zz, yn, cond)
        core(w, s, cond)
    def own(w):
        col(w, z, z < 3, z > 0)
    def step(w, d):
        cl = z - d >= 0
        @pl.when(cl)
        def _(): waitr(w, slab(z - d, x, c, y))
        col(w, lax.max(z - d, 0), (z - d >= 0) & (z < 3), None, cl)
        cr = z + d <= 3
        @pl.when(cr)
        def _(): waitr(w, slab(z + d, x, c, y))
        col(w, lax.min(z + d, 3), None, (z + d <= 3) & (z > 0), cr)
    def plane(w, zz, cond=None):
        par = zz % 2
        s = slab(zz, x + (1 - par) * (1 - 2 * x), c, y + par * (1 - 2 * y))
        tgt = dev(z, x + par * (1 - 2 * x), c, y + (1 - par) * (1 - 2 * y))
        def f():
            waitr(w, s)
        if cond is None: f()
        else: pl.when(cond)(f)
        go(w, s, 32 + zz, tgt, cond)
        core(w, s, cond)
    def plane2(w, zz, cond=None):
        par = zz % 2
        for s in (slab(zz, x + par * (1 - 2 * x), c, y + (1 - par) * (1 - 2 * y)), slab(zz, 1 - x, c, 1 - y)):
            def f():
                waitr(w, s)
            if cond is None: f()
            else: pl.when(cond)(f)
            core(w, s, cond)
    for w in range(nw):
        pltpu.make_async_copy(srcs[w], outs[w].at[me], loc_sem.at[w]).start()
    def both(fn, w, d):
        if d == 0: fn(w, z)
        else:
            fn(w, lax.max(z - d, 0), z - d >= 0)
            fn(w, lax.min(z + d, 3), z + d <= 3)
    stages = []
    def st(w, k):
        if k == 0:
            pltpu.make_async_copy(srcs[w], outs[w].at[me], loc_sem.at[w]).wait()
            own(w)
        elif k == 1: step(w, 1); both(plane, w, 0)
        elif k == 2: step(w, 2); both(plane, w, 1); both(plane2, w, 0)
        elif k == 3: step(w, 3); both(plane, w, 2); both(plane2, w, 1)
        elif k == 4: both(plane, w, 3); both(plane2, w, 2)
        elif k == 5: both(plane2, w, 3)
        elif k == 6:
            for zz in range(4):
                for xx in range(2):
                    for yy in range(2):
                        waitr(w, slab(zz, xx, 1 - c, yy))
    for t in range(nw + 6):
        for w in range(nw):
            k = t - w
            if 0 <= k <= 6: st(order[w], k)
    for (w, s, k, d, cond) in pend:
        if cond is None: cp(w, s, k, d).wait_send()
        else:
            @pl.when(cond)
            def _(): cp(w, s, k, d).wait_send()

def kernel(nw, *refs):
    srcs = refs[:nw]; outs = refs[nw:2*nw]; send, recv, loc = refs[2*nw:]
    ag_body(nw, list(range(nw)), srcs, outs, send, recv, loc)

def all_gather(shards, vmem=False):
    nw = len(shards)
    if (lax.axis_size("dp"), lax.axis_size("seq")) != (16, 2):
        return [lax.all_gather(s, ("dp", "seq"), axis=0) for s in shards]
    sp = pl.BlockSpec(memory_space=pltpu.VMEM if vmem else pl.ANY)
    return pl.pallas_call(
        partial(kernel, nw),
        out_shape=[jax.ShapeDtypeStruct((32,) + s.shape, s.dtype) for s in shards],
        in_specs=[pl.BlockSpec(memory_space=pl.ANY)] * nw,
        out_specs=[sp] * nw,
        scratch_shapes=[pltpu.SemaphoreType.DMA((nw, 36)), pltpu.SemaphoreType.DMA((nw, 32)), pltpu.SemaphoreType.DMA((nw,))],
        compiler_params=pltpu.CompilerParams(collective_id=0, has_side_effects=True, vmem_limit_bytes=60 * 2**20),
    )(*shards)


EPSILON = 1e-05
NEGATIVE = -1e30
DILATIONS = (1, 2, 4)


def layer_norm(features, gain_vec):
    row_mean = jnp.mean(features, axis=-1, keepdims=True)
    centred = features - row_mean
    row_var = jnp.mean(centred * centred, axis=-1, keepdims=True)
    return centred * lax.rsqrt(row_var + EPSILON) * gain_vec


def norm_back(features, gain_vec, grad_normed):
    normed_out, pullback = jax.vjp(layer_norm, features, gain_vec)
    return pullback(grad_normed)


def matmul(left_op, right_op):
    return jnp.dot(left_op, right_op, preferred_element_type=jnp.float32)


def outer_sum(left_op, right_op):
    return lax.dot_general(
        left_op, right_op, (((0,), (0,)), ((), ())), preferred_element_type=jnp.float32
    )


def inner_back(left_op, right_op):
    return lax.dot_general(
        left_op, right_op, (((1,), (1,)), ((), ())), preferred_element_type=jnp.float32
    )


def split_vectors(vectors, model_width, ffn_width):
    piece_sizes = (model_width,) * 6 + (ffn_width, ffn_width, model_width)
    pieces = []
    position = 0
    for piece_len in piece_sizes:
        pieces.append(vectors[position : position + piece_len])
        position = position + piece_len
    return pieces


def head_masks(offsets, branch, head_size):
    dilate = DILATIONS[branch]
    chosen = jnp.arange(dilate, dtype=jnp.int32)[:, None] == offsets[branch][None, :]
    return (chosen, jnp.repeat(chosen, head_size, axis=1))


def select_rows(dense_rows, chosen):
    dilate = chosen.shape[0]
    folded = dense_rows.reshape(dense_rows.shape[0] // dilate, dilate, dense_rows.shape[1])
    picked = jnp.where(chosen[None], folded, jnp.zeros((), dense_rows.dtype))
    return jnp.sum(picked, axis=1, dtype=dense_rows.dtype)


def spread_rows(sparse_rows, chosen, filler):
    dilate = chosen.shape[0]
    spread = jnp.where(chosen[None], sparse_rows[:, None, :], filler)
    return spread.reshape(sparse_rows.shape[0] * dilate, sparse_rows.shape[1])


def window_mask(query_rows, key_rows, first_row, key_first, seg_rows):
    row_ids = first_row + jnp.arange(query_rows, dtype=jnp.int32)[:, None]
    col_ids = key_first + jnp.arange(key_rows, dtype=jnp.int32)[None, :]
    return (col_ids <= row_ids) & (col_ids >= 0) & (col_ids // seg_rows == row_ids // seg_rows)


def masked_scores(queries, keys_win, allowed, score_scale):
    query_heads = queries.reshape(queries.shape[0], HEADS, -1)
    key_heads = keys_win.reshape(keys_win.shape[0], HEADS, -1)
    scores = (
        jnp.einsum("qhd,khd->hqk", query_heads, key_heads, preferred_element_type=jnp.float32)
        * score_scale
    )
    return jnp.where(allowed[None], scores, NEGATIVE)


def attend_piece(queries, keys_win, values_win, allowed, score_scale):
    scores = masked_scores(queries, keys_win, allowed, score_scale)
    log_sums = jax.nn.logsumexp(scores, axis=2)
    weights_low = jnp.exp(scores - log_sums[:, :, None]).astype(jnp.bfloat16)
    value_heads = values_win.reshape(values_win.shape[0], HEADS, -1)
    result = jnp.einsum(
        "hqk,khd->qhd", weights_low, value_heads, preferred_element_type=jnp.float32
    )
    return (result.reshape(queries.shape[0], -1), log_sums)


def attend(queries, keys_win, values_win, first_row, key_first, seg_rows, score_scale):
    rows = queries.shape[0]
    allowed = window_mask(rows, keys_win.shape[0], first_row + 0, key_first, seg_rows)
    result, log_sums = attend_piece(queries, keys_win, values_win, allowed, score_scale)
    return (result, log_sums)


def back_piece(
    queries, keys_win, values_win, log_sums, grad_result, grad_log, allowed, score_scale
):
    query_rows = queries.shape[0]
    scores = masked_scores(queries, keys_win, allowed, score_scale)
    probability = jnp.exp(scores - log_sums[:, :, None])
    query_heads = queries.reshape(query_rows, HEADS, -1)
    key_heads = keys_win.reshape(keys_win.shape[0], HEADS, -1)
    value_heads = values_win.reshape(values_win.shape[0], HEADS, -1)
    grad_heads = grad_result.reshape(query_rows, HEADS, -1)
    grad_probs = jnp.einsum(
        "qhd,khd->hqk", grad_heads, value_heads, preferred_element_type=jnp.float32
    )
    row_dot = jnp.sum(probability * grad_probs, axis=2, keepdims=True)
    grad_scores = (probability * (grad_probs - row_dot + grad_log.T[:, :, None])).astype(
        jnp.bfloat16
    )
    grad_query = (
        jnp.einsum("hqk,khd->qhd", grad_scores, key_heads, preferred_element_type=jnp.float32)
        * score_scale
    )
    grad_keys = (
        jnp.einsum("hqk,qhd->khd", grad_scores, query_heads, preferred_element_type=jnp.float32)
        * score_scale
    )
    grad_values = jnp.einsum(
        "hqk,qhd->khd",
        probability.astype(jnp.bfloat16),
        grad_heads,
        preferred_element_type=jnp.float32,
    )
    key_rows = keys_win.shape[0]
    return (
        grad_query.reshape(query_rows, -1),
        grad_keys.reshape(key_rows, -1),
        grad_values.reshape(key_rows, -1),
    )


def attend_back(
    queries,
    keys_win,
    values_win,
    log_sums,
    grad_result,
    grad_log,
    first_row,
    key_first,
    seg_rows,
    score_scale,
):
    rows = queries.shape[0]
    allowed = window_mask(rows, keys_win.shape[0], first_row + 0, key_first, seg_rows)
    query_part, key_part, value_part = back_piece(
        queries, keys_win, values_win, log_sums, grad_result, grad_log, allowed, score_scale
    )
    return (query_part, key_part, value_part)


def per_device(inputs, cotangent, w_qkv, w_out, w_fc1, w_fc2, vectors, offsets):
    seq_count = lax.axis_size("seq")
    seq_index = lax.axis_index("seq")
    seq_len = TOK_BLK * seq_count
    seg_rows = seq_len // 4
    score_scale = HEAD_DIM ** (-0.5)
    shards = (
        w_qkv.astype(jnp.bfloat16),
        w_out.astype(jnp.bfloat16),
        w_fc1.astype(jnp.bfloat16),
        w_fc2.astype(jnp.bfloat16),
        vectors.astype(jnp.bfloat16),
    )

    mine = [
        shards[0].reshape(-1, 3 * D),
        shards[1].reshape(-1, D),
        shards[2].reshape(-1, FF),
        shards[3].reshape(-1, D),
        jnp.broadcast_to(jnp.pad(shards[4].astype(jnp.float32), (0, -shards[4].shape[0] % 128))[None], (8, shards[4].shape[0] + -shards[4].shape[0] % 128)),
    ]
    full = all_gather(mine)
    params = (
        full[0].reshape(D, 3 * D),
        full[1].reshape(D, D),
        full[2].reshape(D, FF),
        full[3].reshape(FF, D),
        full[4][:, 0, : shards[4].shape[0]].reshape(-1),
    )

    selectors = [head_masks(offsets, branch, HEAD_DIM) for branch in range(3)]
    plans = []
    for branch in range(3):
        block_rows = TOK_BLK // DILATIONS[branch]
        window = max(seg_rows, block_rows)
        first_row = seq_index * block_rows
        plans.append((first_row, block_rows, window, first_row + block_rows - window))
    totals = None
    layer_rows = []
    grad_rows = []
    for micro_batch in range(MB):
        qkv_weight, out_weight, up_weight, down_weight, vector_vals = params
        (
            gain_in,
            bias_query,
            bias_value,
            gain_attn,
            bias_out,
            gain_mid,
            bias_up,
            gain_ffn,
            bias_down,
        ) = split_vectors(vector_vals, D, FF)
        tokens = inputs[micro_batch, 0].astype(jnp.float32)
        normed = layer_norm(tokens, gain_in).astype(jnp.bfloat16)
        bias_full = jnp.concatenate([bias_query, jnp.zeros_like(bias_query), bias_value])
        qkv_rows = (matmul(normed, qkv_weight) + bias_full).astype(jnp.bfloat16)
        sparse_query = [select_rows(qkv_rows[:, :D], selectors[branch][1]) for branch in range(3)]
        sparse_keys = [
            select_rows(qkv_rows[:, D : 2 * D], selectors[branch][1]) for branch in range(3)
        ]
        sparse_values = [
            select_rows(qkv_rows[:, 2 * D :], selectors[branch][1]) for branch in range(3)
        ]
        windows = []
        gathered = (
            lax.all_gather(sparse_keys[0], "seq", axis=0, tiled=True),
            lax.all_gather(sparse_values[0], "seq", axis=0, tiled=True),
            lax.all_gather(sparse_keys[1], "seq", axis=0, tiled=True),
            lax.all_gather(sparse_values[1], "seq", axis=0, tiled=True),
            lax.all_gather(sparse_keys[2], "seq", axis=0, tiled=True),
            lax.all_gather(sparse_values[2], "seq", axis=0, tiled=True),
        )
        for branch in range(3):
            first_row, block_rows, window, start = plans[branch]
            begin = jnp.maximum(start, 0)
            windows.append(
                (
                    lax.dynamic_slice_in_dim(gathered[2 * branch], begin, window, 0),
                    lax.dynamic_slice_in_dim(gathered[2 * branch + 1], begin, window, 0),
                    begin,
                )
            )
        branch_outs = []
        branch_logs = []
        sparse_logs = []
        for branch in range(3):
            keys_win, values_win, key_first = windows[branch]
            result, log_sums = attend(
                sparse_query[branch],
                keys_win,
                values_win,
                plans[branch][0],
                key_first,
                seg_rows,
                score_scale,
            )
            sparse_logs.append(log_sums)
            branch_outs.append(
                spread_rows(result, selectors[branch][1], 0.0).reshape(TOK_BLK, HEADS, HEAD_DIM)
            )
            branch_logs.append(spread_rows(log_sums.T, selectors[branch][0], NEGATIVE))
        stacked = jnp.stack(branch_logs)
        total_log = jax.nn.logsumexp(stacked, axis=0)
        mixing = jnp.exp(stacked - total_log[None])
        mixed = sum(
            (mixing[branch][:, :, None] * branch_outs[branch] for branch in range(3))
        ).reshape(TOK_BLK, D)
        inner = layer_norm(mixed, gain_attn).astype(jnp.bfloat16)
        middle = tokens + (matmul(inner, out_weight) + bias_out)
        normed_mid = layer_norm(middle, gain_mid).astype(jnp.bfloat16)
        hidden = matmul(normed_mid, up_weight) + bias_up
        active, gelu_back = jax.vjp(partial(jax.nn.gelu, approximate=False), hidden)
        inner_ffn = layer_norm(active, gain_ffn).astype(jnp.bfloat16)
        layer_rows.append(
            (middle + (matmul(inner_ffn, down_weight) + bias_down)).astype(jnp.bfloat16)
        )
        grad_layer = cotangent[micro_batch, 0].astype(jnp.float32)
        grad_down = grad_layer.astype(jnp.bfloat16)
        grad_inner_ffn = inner_back(grad_down, down_weight)
        grad_active, grad_gain_ffn = norm_back(active, gain_ffn, grad_inner_ffn)
        grad_hidden = gelu_back(grad_active)[0].astype(jnp.bfloat16)
        grad_normed_mid = inner_back(grad_hidden, up_weight)
        grad_middle_part, grad_gain_mid = norm_back(middle, gain_mid, grad_normed_mid)
        grad_middle = grad_layer + grad_middle_part
        grad_branch = grad_middle.astype(jnp.bfloat16)
        grad_inner = inner_back(grad_branch, out_weight)
        grad_mixed, grad_gain_attn = norm_back(mixed, gain_attn, grad_inner)
        grad_heads = grad_mixed.reshape(TOK_BLK, HEADS, HEAD_DIM)
        along_out = [jnp.sum(grad_heads * branch_outs[branch], axis=2) for branch in range(3)]
        common = sum((mixing[branch] * along_out[branch] for branch in range(3)))
        grad_query_dense = jnp.zeros((TOK_BLK, D), jnp.float32)
        key_terms = []
        for branch in range(3):
            chosen, wide_mask = selectors[branch]
            keys_win, values_win, key_first = windows[branch]
            grad_result = select_rows(
                (mixing[branch][:, :, None] * grad_heads).reshape(TOK_BLK, D), wide_mask
            ).astype(jnp.bfloat16)
            grad_log = select_rows(mixing[branch] * (along_out[branch] - common), chosen)
            query_part, key_part, value_part = attend_back(
                sparse_query[branch],
                keys_win,
                values_win,
                sparse_logs[branch],
                grad_result,
                grad_log,
                plans[branch][0],
                key_first,
                seg_rows,
                score_scale,
            )
            grad_query_dense = grad_query_dense + spread_rows(query_part, wide_mask, 0.0)
            key_terms.append(key_part)
            key_terms.append(value_part)
        full_terms = []
        for branch in range(3):
            full_rows = seq_len // DILATIONS[branch]
            for member in range(2):
                empty = jnp.zeros((full_rows, D), jnp.float32)
                full_terms.append(
                    lax.dynamic_update_slice_in_dim(
                        empty, key_terms[2 * branch + member], windows[branch][2], 0
                    )
                )
        owned_keys = (
            lax.psum_scatter(
                full_terms[0].astype(jnp.bfloat16), "seq", scatter_dimension=0, tiled=True
            ).astype(jnp.float32),
            lax.psum_scatter(
                full_terms[1].astype(jnp.bfloat16), "seq", scatter_dimension=0, tiled=True
            ).astype(jnp.float32),
            lax.psum_scatter(
                full_terms[2].astype(jnp.bfloat16), "seq", scatter_dimension=0, tiled=True
            ).astype(jnp.float32),
            lax.psum_scatter(
                full_terms[3].astype(jnp.bfloat16), "seq", scatter_dimension=0, tiled=True
            ).astype(jnp.float32),
            lax.psum_scatter(
                full_terms[4].astype(jnp.bfloat16), "seq", scatter_dimension=0, tiled=True
            ).astype(jnp.float32),
            lax.psum_scatter(
                full_terms[5].astype(jnp.bfloat16), "seq", scatter_dimension=0, tiled=True
            ).astype(jnp.float32),
        )
        grad_keys_dense = sum(
            (spread_rows(owned_keys[2 * branch], selectors[branch][1], 0.0) for branch in range(3))
        )
        grad_values_dense = sum(
            (
                spread_rows(owned_keys[2 * branch + 1], selectors[branch][1], 0.0)
                for branch in range(3)
            )
        )
        grad_qkv_rows = jnp.concatenate(
            [grad_query_dense, grad_keys_dense, grad_values_dense], axis=1
        ).astype(jnp.bfloat16)
        grad_bias_query = jnp.sum(grad_qkv_rows[:, :D].astype(jnp.float32), axis=0)
        grad_bias_value = jnp.sum(grad_qkv_rows[:, 2 * D :].astype(jnp.float32), axis=0)
        grad_normed = inner_back(grad_qkv_rows, qkv_weight)
        grad_input_part, grad_gain_in = norm_back(tokens, gain_in, grad_normed)
        grad_rows.append(grad_middle + grad_input_part)
        vector_grad = jnp.concatenate(
            [
                grad_gain_in,
                grad_bias_query,
                grad_bias_value,
                grad_gain_attn,
                jnp.sum(grad_branch.astype(jnp.float32), axis=0),
                grad_gain_mid,
                jnp.sum(grad_hidden.astype(jnp.float32), axis=0),
                grad_gain_ffn,
                jnp.sum(grad_down.astype(jnp.float32), axis=0),
            ]
        )
        micro_grads = (
            outer_sum(normed, grad_qkv_rows),
            outer_sum(inner, grad_branch),
            outer_sum(normed_mid, grad_hidden),
            outer_sum(inner_ffn, grad_down),
            vector_grad,
        )
        if totals is None:
            totals = micro_grads
        else:
            totals = tuple(
                (total_sum + grad_one for total_sum, grad_one in zip(totals, micro_grads))
            )
    owned_grads = (
        lax.psum_scatter(totals[0].reshape(-1), ("dp", "seq"), scatter_dimension=0, tiled=True),
        lax.psum_scatter(totals[1].reshape(-1), ("dp", "seq"), scatter_dimension=0, tiled=True),
        lax.psum_scatter(totals[2].reshape(-1), ("dp", "seq"), scatter_dimension=0, tiled=True),
        lax.psum_scatter(totals[3].reshape(-1), ("dp", "seq"), scatter_dimension=0, tiled=True),
        lax.psum_scatter(totals[4], ("dp", "seq"), scatter_dimension=0, tiled=True),
    )
    layer_out = jnp.stack(layer_rows)[:, None]
    input_grad = jnp.stack(grad_rows)[:, None]
    return (
        layer_out,
        input_grad,
        owned_grads[0],
        owned_grads[1],
        owned_grads[2],
        owned_grads[3],
        owned_grads[4],
    )


def solution(mesh):
    return jax.shard_map(
        per_device,
        mesh=mesh,
        in_specs=(
            P(None, "dp", "seq", None),
            P(None, "dp", "seq", None),
            P(("dp", "seq")),
            P(("dp", "seq")),
            P(("dp", "seq")),
            P(("dp", "seq")),
            P(("dp", "seq")),
            P(),
        ),
        out_specs=(
            P(None, "dp", "seq", None),
            P(None, "dp", "seq", None),
            P(("dp", "seq")),
            P(("dp", "seq")),
            P(("dp", "seq")),
            P(("dp", "seq")),
            P(("dp", "seq")),
        ),
        check_vma=False,
    )
```
